1024 devices in a mesh: dp: 8 (over x), group: 8 (over y), local: 16 (over z, core).
Axes of the slice: x: 8, y: 8, z: 8, core: 2. Of those that a mesh axis runs over, the one named last changes fastest.
Arguments:
- tokens: bfloat16 [16384, 1024], P(('dp', 'group', 'local')), may hold values from -6 to 6
- cotangent: bfloat16 [16384, 1024], P(('dp', 'group', 'local')), may hold values from -6 to 6
- expert_ids: int32 [16384, 8], P(('dp', 'group', 'local')), may hold values from 0 to 127, as said below
- router_weights: bfloat16 [16384, 8], P(('dp', 'group', 'local')), may hold values from 0.049804688 to 1
- gate_weight: bfloat16 [128, 1024, 384], P(('group', 'local'), 'dp'), may hold values from -0.1875 to 0.1875
- up_weight: bfloat16 [128, 1024, 384], P(('group', 'local'), 'dp'), may hold values from -0.1875 to 0.1875
- down_weight: bfloat16 [128, 384, 1024], P(('group', 'local'), None, 'dp'), may hold values from -0.3125 to 0.3125
Outputs:
- layer_output: bfloat16 [16384, 1024], P(('dp', 'group', 'local'))
- token_grads: bfloat16 [16384, 1024], P(('dp', 'group', 'local'))
- router_grads: bfloat16 [16384, 8], P(('dp', 'group', 'local'))
- gate_grad: bfloat16 [128, 1024, 384], P(('group', 'local'), 'dp')
- up_grad: bfloat16 [128, 1024, 384], P(('group', 'local'), 'dp')
- down_grad: bfloat16 [128, 384, 1024], P(('group', 'local'), None, 'dp')
The draws below stay inside these ranges and needn't reach their ends.
Inputs may be any that keep to these rules, and one draw needn't show every extreme that they name: `expert_ids`: expert e belongs to group e // 16. Columns 2j and 2j+1 of a token name two different experts of one group, and the 4 column pairs of a token name 4 different groups. Every device sends exactly 8 of its tokens to each group. For every dp index and group, one expert of the group is named by exactly 3 of the tokens that each device of that dp index sends to the group, and every other expert of the group by fewer; so at most 24 tokens reach one expert from the devices of one dp index and one local index, and that many reach the busiest one.
All inputs are finite; a program needn't handle non-finite values.
Results may differ from the reference program's by a relative error of at most 0.013.
Values may be sent and summed in bfloat16 or wider, within the bound.
No kernel may reach another device: no remote copies, remote signals or barrier semaphores. Data moves between devices by JAX's collectives and lax.ppermute only.
A program may use at most 32 MiB of HBM per device.

```python
import math
import jax
import jax.numpy as jnp
from jax import lax

D = 1024
FF = 384
TOPK = 8
GROUPS_TOK = 4
TOK_DEV = 16
EXPERTS = 128
TOKENS = 16384
OWNER_CAP = 24
N_DP = 8
N_GROUP = 8
N_LOCAL = 16


def draw_expert_ids(key, part):
    devices = N_DP * N_GROUP * N_LOCAL
    per_group = TOK_DEV * GROUPS_TOK // N_GROUP
    hot_rows = min(per_group, 6 * per_group // N_LOCAL)
    others = N_LOCAL - 1
    stride = N_GROUP // GROUPS_TOK
    key_group, key_token, key_hot, key_block, key_other = jax.random.split(jax.random.fold_in(key, 7), 5)
    group_perm = jax.vmap(lambda subkey: jax.random.permutation(subkey, N_GROUP))(jax.random.split(key_group, devices))
    token_perm = jax.vmap(lambda subkey: jax.random.permutation(subkey, TOK_DEV))(jax.random.split(key_token, devices))
    hot_local = jax.random.randint(key_hot, (N_DP, N_GROUP), 0, N_LOCAL)
    block_perm = jax.vmap(lambda subkey: jax.random.permutation(subkey, per_group))(jax.random.split(key_block, devices * N_GROUP))
    block_perm = block_perm.reshape(devices, N_GROUP, per_group)
    other_perm = jax.vmap(lambda subkey: jax.random.permutation(subkey, others))(jax.random.split(key_other, devices * N_GROUP))
    other_perm = other_perm.reshape(devices, N_GROUP, others)
    device = jnp.arange(devices)[:, None, None]
    column = jnp.arange(GROUPS_TOK)[None, None, :]
    placed = token_perm[:, :, None]
    residue = (placed + column * stride) % N_GROUP
    group_index = group_perm[device, residue]
    within = column * (TOK_DEV // N_GROUP) + placed // N_GROUP
    position = block_perm[device, group_index, within]
    hot_label = hot_local[device // (N_GROUP * N_LOCAL), group_index]

    def label_at(slot_index):
        other_label = other_perm[device, group_index, jnp.maximum(slot_index - hot_rows, 0) % others]
        other_label = other_label + (other_label >= hot_label).astype(jnp.int32)
        return jnp.where(slot_index < hot_rows, hot_label, other_label)
    first_expert = group_index * N_LOCAL + label_at(position)
    second = group_index * N_LOCAL + label_at(position + per_group)
    return jnp.stack([first_expert, second], axis=3).reshape(devices * TOK_DEV, 2 * GROUPS_TOK).astype(jnp.int32)


def block_levels(rng, dims, cuts, low, largest):
    level = 1.0
    for axis_at, shards_of in cuts:
        heights = jax.random.uniform(jax.random.fold_in(jax.random.fold_in(rng, 6), axis_at), (shards_of,), jnp.float32, low / len(cuts), largest / len(cuts))
        level = level * jnp.repeat(jnp.exp(heights), dims[axis_at] // shards_of).reshape((-1,) + (1,) * (len(dims) - 1 - axis_at))
    return level


def scatter_about(stream_key, shape, deviation, limit, shards=(), kind=jnp.bfloat16):
    level = block_levels(stream_key, shape, shards, -0.22, 0.18) if shards else 1.0
    array = jax.random.normal(stream_key, shape, jnp.float32) * deviation * level
    return jnp.minimum(jnp.maximum(array, -limit), limit).astype(kind)


def setup_inputs(seed: int = 0) -> dict:
    splits = jax.random.split(jax.random.key(seed), 8)
    return {
        "tokens": scatter_about(splits[0], (TOKENS, D), 1.0, 6.0, ((0, 1024),)),
        "cotangent": scatter_about(splits[1], (TOKENS, D), 1.0, 6.0, ((0, 1024),)),
        "expert_ids": draw_expert_ids(jax.random.fold_in(splits[7], 71), 0),
        "router_weights": jnp.clip(jnp.exp(math.log(1.0) - 2.9996462 * jax.random.uniform(splits[3], (TOKENS, TOPK), jnp.float32) ** block_levels(splits[3], (TOKENS, TOPK), ((0, 1024),), -0.2, 0.2)), 0.049804688, 1.0).astype(jnp.bfloat16),
        "gate_weight": scatter_about(splits[4], (EXPERTS, D, FF), D ** -0.5, 0.1875, ((0, 128), (1, 8))),
        "up_weight": scatter_about(splits[5], (EXPERTS, D, FF), D ** -0.5, 0.1875, ((0, 128), (1, 8))),
        "down_weight": scatter_about(splits[6], (EXPERTS, FF, D), FF ** -0.5, 0.3125, ((0, 128), (2, 8))),
    }


def rounded(value):
    return lax.optimization_barrier(value.astype(jnp.bfloat16)).astype(jnp.float32)


def expert_pass(rows_in, grad_out, gate_full, up_full, down_full):
    gate_pre = jnp.dot(rows_in, gate_full, preferred_element_type=jnp.float32)
    up_pre = jnp.dot(rows_in, up_full, preferred_element_type=jnp.float32)
    sigmoid_gate = jax.nn.sigmoid(gate_pre)
    hidden = (gate_pre * sigmoid_gate * up_pre).astype(jnp.bfloat16)
    expert_out = jnp.dot(hidden, down_full, preferred_element_type=jnp.float32).astype(jnp.bfloat16)
    hidden_grad = jnp.dot(grad_out, down_full.T, preferred_element_type=jnp.float32)
    gate_pre_grad = (hidden_grad * up_pre * sigmoid_gate * (1.0 + gate_pre * (1.0 - sigmoid_gate))).astype(jnp.bfloat16)
    up_pre_grad = (hidden_grad * gate_pre * sigmoid_gate).astype(jnp.bfloat16)
    expert_in_grad = (jnp.dot(gate_pre_grad, gate_full.T, preferred_element_type=jnp.float32)
                      + jnp.dot(up_pre_grad, up_full.T, preferred_element_type=jnp.float32)).astype(jnp.bfloat16)
    gate_term = jnp.dot(rows_in.T, gate_pre_grad, preferred_element_type=jnp.float32)
    up_term = jnp.dot(rows_in.T, up_pre_grad, preferred_element_type=jnp.float32)
    down_term = jnp.dot(hidden.T, grad_out, preferred_element_type=jnp.float32)
    return expert_out, expert_in_grad, gate_term, up_term, down_term


def reference(tokens, cotangent, expert_ids, router_weights, gate_weight, up_weight, down_weight):
    assign_count = TOKENS * TOPK
    row_limit = N_LOCAL * OWNER_CAP
    flat_expert = expert_ids.reshape(-1).astype(jnp.int32)
    token_index = jnp.arange(assign_count, dtype=jnp.int32) // TOPK
    slice_index = token_index // (TOKENS // N_DP)
    sort_keys = flat_expert * N_DP + slice_index
    sorted_index = jnp.argsort(sort_keys, stable=True).astype(jnp.int32)
    cell_counts = jax.ops.segment_sum(jnp.ones((assign_count,), jnp.int32), sort_keys, num_segments=EXPERTS * N_DP)
    cell_starts = (jnp.cumsum(cell_counts) - cell_counts).astype(jnp.int32)
    padded_index = jnp.concatenate([sorted_index, jnp.full((row_limit,), assign_count, jnp.int32)])
    token_table = jnp.concatenate([tokens, jnp.zeros((1, D), tokens.dtype)])
    grad_table = jnp.concatenate([cotangent, jnp.zeros((1, D), cotangent.dtype)])
    scale_table = jnp.concatenate([router_weights.reshape(-1), jnp.zeros((1,), router_weights.dtype)])

    def expert_step(state_pair, expert):
        gate_full = gate_weight[expert]
        up_full = up_weight[expert]
        down_full = down_weight[expert]

        def slice_step(loop_state, data_index):
            outputs_all, grads_all, gate_sum, up_sum, down_sum = loop_state
            cell_index = expert * N_DP + data_index
            entries = lax.dynamic_slice_in_dim(padded_index, cell_starts[cell_index], row_limit)
            entries = jnp.where(jnp.arange(row_limit, dtype=jnp.int32) < cell_counts[cell_index], entries, assign_count)
            row_tokens = entries // TOPK
            rows_in = token_table[row_tokens]
            scale_rows = scale_table[entries].astype(jnp.float32)
            grad_out = (scale_rows[:, None] * grad_table[row_tokens].astype(jnp.float32)).astype(jnp.bfloat16)
            expert_out, expert_in_grad, gate_term, up_term, down_term = expert_pass(rows_in, grad_out, gate_full, up_full, down_full)
            outputs_all = outputs_all.at[entries].set(expert_out)
            grads_all = grads_all.at[entries].set(expert_in_grad)
            gate_sum = gate_sum + rounded(gate_term)
            up_sum = up_sum + rounded(up_term)
            down_sum = down_sum + rounded(down_term)
            return (outputs_all, grads_all, gate_sum, up_sum, down_sum), None

        outputs_all, grads_all = state_pair
        start_state = (outputs_all, grads_all, jnp.zeros((D, FF), jnp.float32),
                       jnp.zeros((D, FF), jnp.float32), jnp.zeros((FF, D), jnp.float32))
        final_state, _ = lax.scan(slice_step, start_state, jnp.arange(N_DP, dtype=jnp.int32))
        outputs_all, grads_all, gate_sum, up_sum, down_sum = final_state
        return (outputs_all, grads_all), (gate_sum.astype(jnp.bfloat16), up_sum.astype(jnp.bfloat16), down_sum.astype(jnp.bfloat16))

    start_pair = (jnp.zeros((assign_count + 1, D), jnp.bfloat16), jnp.zeros((assign_count + 1, D), jnp.bfloat16))
    final_pair, stacked = lax.scan(expert_step, start_pair, jnp.arange(EXPERTS, dtype=jnp.int32))
    outputs_all, grads_all = final_pair
    gate_grad, up_grad, down_grad = stacked
    expert_out = outputs_all[:assign_count].reshape(TOKENS, GROUPS_TOK, 2, D).astype(jnp.float32)
    expert_in_grad = grads_all[:assign_count].reshape(TOKENS, GROUPS_TOK, 2, D).astype(jnp.float32)
    scales = router_weights.reshape(TOKENS, GROUPS_TOK, 2).astype(jnp.float32)
    group_out = rounded(jnp.sum(scales[..., None] * expert_out, axis=2))
    layer_output = jnp.sum(group_out, axis=1).astype(jnp.bfloat16)
    group_grad = rounded(jnp.sum(expert_in_grad, axis=2))
    token_grads = jnp.sum(group_grad, axis=1).astype(jnp.bfloat16)
    router_grads = jnp.sum(cotangent.astype(jnp.float32)[:, None, None, :] * expert_out, axis=3)
    router_grads = router_grads.reshape(TOKENS, TOPK).astype(jnp.bfloat16)
    return layer_output, token_grads, router_grads, gate_grad, up_grad, down_grad
```

```python
import jax
import jax.numpy as jnp
from jax import lax
from jax.experimental import pallas as pl
from jax.experimental.pallas import tpu as pltpu
from jax.sharding import PartitionSpec as P

INTERPRET = False
BF16 = jnp.bfloat16
F32 = jnp.float32
LANES = 128
CAP = 3


def vmem():
    return pl.BlockSpec(memory_space=pltpu.VMEM)


def dot(a, b, dims=((1,), (0,))):
    return lax.dot_general(a, b, (dims, ((), ())), preferred_element_type=F32)


def spread_rows(wide, rows, first, blocks):
    n, features = wide.shape
    per = features // LANES
    for c in range(per):
        rows[pl.ds(first + c, n, stride=blocks), :] = wide[:, c * LANES : (c + 1) * LANES]


def gather_rows(rows, n, first, blocks, per):
    return jnp.concatenate(
        [rows[pl.ds(first + c, n, stride=blocks), :] for c in range(per)], axis=1
    )


def token_ranks(ids, experts):
    tokens, columns = ids.shape
    lane = lax.broadcasted_iota(jnp.int32, (tokens, experts), 1)
    matches = [ids[:, k : k + 1] == lane for k in range(columns)]
    named = jnp.zeros((tokens, experts), F32)
    for match in matches:
        named = named + match.astype(F32)
    row = lax.broadcasted_iota(jnp.int32, (tokens, tokens), 0)
    column = lax.broadcasted_iota(jnp.int32, (tokens, tokens), 1)
    earlier = (column < row).astype(F32).astype(BF16)
    return matches, named, dot(earlier, named.astype(BF16))


def pack_kernel(gate, up, down, out):
    features, hidden = gate.shape
    for i, weight in enumerate((gate, up)):
        for c in range(hidden // LANES):
            at = i * hidden + c * LANES
            out[at : at + features, :] = weight[:, c * LANES : (c + 1) * LANES]
    out[2 * hidden :, :] = down[...]


def send_kernel(tokens, cotangent, ids, weights, out, rows):
    experts = out.shape[0] // (2 * CAP * tokens.shape[1] // LANES)
    per = tokens.shape[1] // LANES
    blocks = 2 * CAP * per
    matches, named, rank = token_ranks(ids[...], experts)
    scale = jnp.zeros(named.shape, F32)
    values = weights[...].astype(F32)
    for k, match in enumerate(matches):
        scale = scale + jnp.where(match, values[:, k : k + 1], 0.0)
    for r in range(CAP):
        here = (named > 0.0) & (rank == float(r))
        pick = jnp.where(here, 1.0, 0.0).astype(BF16)
        scaled = jnp.where(here, scale, 0.0).astype(BF16)
        spread_rows(dot(pick, tokens[...], ((0,), (0,))), rows, r * per, blocks)
        spread_rows(dot(scaled, cotangent[...], ((0,), (0,))), rows, (CAP + r) * per, blocks)
    out[...] = rows[...].astype(BF16)


def expert_kernel(recv, gathered, back, terms, rows, gate_up, down, sems):
    peers = gathered.shape[0]
    features = gate_up.shape[0] // peers
    hidden = down.shape[0]
    width = gate_up.shape[0]
    per = width // LANES
    blocks = 2 * CAP * per
    sources = recv.shape[0] // blocks
    copies = []
    for d in range(peers):
        for i in range(2 * hidden // LANES):
            copies.append(
                pltpu.make_async_copy(
                    gathered.at[d, pl.ds(i * LANES, LANES), :],
                    gate_up.at[pl.ds(d * features, features), pl.ds(i * LANES, LANES)],
                    sems.at[0, d * (2 * hidden // LANES) + i],
                )
            )
    late = [
        pltpu.make_async_copy(
            gathered.at[d, pl.ds(2 * hidden, hidden), :],
            down.at[:, pl.ds(d * features, features)],
            sems.at[1, d],
        )
        for d in range(peers)
    ]
    for copy in copies + late:
        copy.start()
    rows[...] = recv[...].astype(F32)
    x = jnp.concatenate(
        [gather_rows(rows, sources, r * per, blocks, per).astype(BF16) for r in range(CAP)], axis=0
    )
    g = jnp.concatenate(
        [gather_rows(rows, sources, (CAP + r) * per, blocks, per).astype(BF16) for r in range(CAP)],
        axis=0,
    )
    for copy in copies:
        copy.wait()
    pre = dot(x, gate_up[...])
    gate_pre, up_pre = pre[:, :hidden], pre[:, hidden:]
    sigmoid = 1.0 / (1.0 + jnp.exp(-gate_pre))
    inner = (gate_pre * sigmoid * up_pre).astype(BF16)
    for copy in late:
        copy.wait()
    hidden_grad = dot(g, down[...], ((1,), (1,)))
    out = dot(inner, down[...])
    for r in range(CAP):
        spread_rows(out[r * sources : (r + 1) * sources], rows, r * per, blocks)
    gate_grad = (hidden_grad * up_pre * sigmoid * (1.0 + gate_pre * (1.0 - sigmoid))).astype(BF16)
    up_grad = (hidden_grad * gate_pre * sigmoid).astype(BF16)
    both = jnp.concatenate([gate_grad, up_grad], axis=1)
    back_grad = dot(both, gate_up[...], ((1,), (1,)))
    for r in range(CAP):
        spread_rows(back_grad[r * sources : (r + 1) * sources], rows, (CAP + r) * per, blocks)
    back[...] = rows[...].astype(BF16)
    down_term = dot(inner, g, ((0,), (0,))).astype(BF16)
    for d in range(peers):
        terms[d, 2 * hidden :, :] = down_term[:, d * features : (d + 1) * features]
    term = dot(x, both, ((0,), (0,))).astype(BF16)
    for d in range(peers):
        for i in range(2 * hidden // LANES):
            terms[d, i * LANES : (i + 1) * LANES, :] = term[
                d * features : (d + 1) * features, i * LANES : (i + 1) * LANES
            ]


def combine_kernel(back, cotangent, ids, weights, layer, token_grads, router_grads, rows):
    tokens, width = cotangent.shape
    columns = ids.shape[1]
    per = width // LANES
    blocks = 2 * CAP * per
    experts = back.shape[0] // blocks
    rows[...] = back[...].astype(F32)
    matches, named, rank = token_ranks(ids[...], experts)
    ranks = [rank == float(r) for r in range(CAP)]
    pick = jnp.concatenate(
        [
            jnp.concatenate(
                [jnp.where(match & at, 1.0, 0.0) for at in ranks],
                axis=1,
            )
            for match in matches
        ],
        axis=0,
    ).astype(BF16)
    outs = jnp.concatenate(
        [gather_rows(rows, experts, r * per, blocks, per).astype(BF16) for r in range(CAP)], axis=0
    )
    grads = jnp.concatenate(
        [
            gather_rows(rows, experts, (CAP + r) * per, blocks, per).astype(BF16)
            for r in range(CAP)
        ],
        axis=0,
    )
    out = dot(pick, outs)
    grad = dot(pick, grads)
    values = weights[...].astype(F32)
    cot = cotangent[...].astype(F32)
    lane = lax.broadcasted_iota(jnp.int32, (tokens, columns), 1)
    total = jnp.zeros((tokens, width), F32)
    total_grad = jnp.zeros((tokens, width), F32)
    routed = jnp.zeros((tokens, columns), F32)
    for j in range(columns // 2):
        a, b = 2 * j, 2 * j + 1
        first, second = out[a * tokens : (a + 1) * tokens], out[b * tokens : (b + 1) * tokens]
        pair = values[:, a : a + 1] * first + values[:, b : b + 1] * second
        total = total + pair.astype(BF16).astype(F32)
        pair = grad[a * tokens : (a + 1) * tokens] + grad[b * tokens : (b + 1) * tokens]
        total_grad = total_grad + pair.astype(BF16).astype(F32)
        routed = jnp.where(lane == a, jnp.sum(cot * first, axis=1, keepdims=True), routed)
        routed = jnp.where(lane == b, jnp.sum(cot * second, axis=1, keepdims=True), routed)
    layer[...] = total.astype(BF16)
    token_grads[...] = total_grad.astype(BF16)
    router_grads[...] = routed.astype(BF16)


def unpack_kernel(lines, gate, up, down):
    features, hidden = gate.shape
    for i, weight in enumerate((gate, up)):
        for c in range(hidden // LANES):
            at = i * hidden + c * LANES
            weight[:, c * LANES : (c + 1) * LANES] = lines[at : at + features, :]
    down[...] = lines[2 * hidden :, :]


def call(kernel, outs, scratch=(), in_specs=None, name=None):
    shapes = [jax.ShapeDtypeStruct(shape, BF16) for shape in outs]
    single = len(shapes) == 1
    return pl.pallas_call(
        kernel,
        out_shape=shapes[0] if single else shapes,
        in_specs=in_specs,
        out_specs=vmem() if single else [vmem() for _ in shapes],
        scratch_shapes=list(scratch),
        interpret=INTERPRET,
        name=name,
    )


def pack_weights(gate, up, down):
    hidden = gate.shape[1]
    return call(pack_kernel, [(3 * hidden, LANES)], in_specs=[vmem()] * 3, name="pack_weights")(
        gate, up, down
    )


def send_rows(tokens, cotangent, ids, weights, experts):
    lines = experts * 2 * CAP * tokens.shape[1] // LANES
    return call(
        send_kernel,
        [(lines, LANES)],
        scratch=[pltpu.VMEM((lines, LANES), F32)],
        in_specs=[vmem()] * 4,
        name="send_rows",
    )(tokens, cotangent, ids, weights)


def expert(recv, gathered, hidden, width):
    peers = gathered.shape[0]
    return call(
        expert_kernel,
        [recv.shape, gathered.shape],
        scratch=[
            pltpu.VMEM(recv.shape, F32),
            pltpu.VMEM((width, 2 * hidden), BF16),
            pltpu.VMEM((hidden, width), BF16),
            pltpu.SemaphoreType.DMA((2, peers * 2 * hidden // LANES)),
        ],
        in_specs=[vmem(), pl.BlockSpec(memory_space=pl.ANY)],
        name="expert",
    )(recv, gathered)


def combine(back, cotangent, ids, weights):
    return call(
        combine_kernel,
        [cotangent.shape, cotangent.shape, ids.shape],
        scratch=[pltpu.VMEM(back.shape, F32)],
        in_specs=[vmem()] * 4,
        name="combine",
    )(back, cotangent, ids, weights)


def unpack_grads(lines, features, hidden):
    return call(
        unpack_kernel,
        [(features, hidden), (features, hidden), (hidden, LANES)],
        in_specs=[vmem()],
        name="unpack_grads",
    )(lines)


def exchange(lines, peers):
    out = lax.all_to_all(
        lines.reshape(peers, -1, LANES), ("group", "local"), split_axis=0, concat_axis=0, tiled=True
    )
    return out.reshape(lines.shape)


def local(tokens, cotangent, expert_ids, router_weights, gate_weight, up_weight, down_weight):
    experts = lax.axis_size("group") * lax.axis_size("local")
    peers = lax.axis_size("dp")
    features, hidden = gate_weight.shape[1:]
    width = tokens.shape[1]
    packed = pack_weights(gate_weight[0], up_weight[0], down_weight[0])
    gathered = lax.all_gather(packed, "dp", axis=0, tiled=True).reshape(peers, -1, LANES)
    sent = send_rows(tokens, cotangent, expert_ids, router_weights, experts)
    recv = exchange(sent, experts)
    back, terms = expert(recv, gathered, hidden, width)
    scattered = lax.psum_scatter(terms.reshape(-1, LANES), "dp", tiled=True)
    returned = exchange(back, experts)
    layer, token_grads, router_grads = combine(returned, cotangent, expert_ids, router_weights)
    gate, up, down = unpack_grads(scattered, features, hidden)
    return layer, token_grads, router_grads, gate[None], up[None], down[None]


def solution(mesh):
    tokens = P(("dp", "group", "local"), None)
    rows = P(("group", "local"), "dp", None)
    columns = P(("group", "local"), None, "dp")
    return jax.shard_map(
        local,
        mesh=mesh,
        in_specs=(tokens, tokens, tokens, tokens, rows, rows, columns),
        out_specs=(tokens, tokens, tokens, rows, rows, columns),
        check_vma=False,
    )
```

```python
import jax
import jax.numpy as jnp
from jax import lax
from jax.experimental import pallas as pl
from jax.experimental.pallas import tpu as pltpu
from jax.sharding import PartitionSpec as P

INTERPRET = False
BF16 = jnp.bfloat16
F32 = jnp.float32
LANES = 128
CAP = 3


def vmem():
    return pl.BlockSpec(memory_space=pltpu.VMEM)


def dot(a, b, dims=((1,), (0,))):
    return lax.dot_general(a, b, (dims, ((), ())), preferred_element_type=F32)


def spread_rows(wide, rows, first, blocks):
    n, features = wide.shape
    per = features // LANES
    for c in range(per):
        rows[pl.ds(first + c, n, stride=blocks), :] = wide[:, c * LANES : (c + 1) * LANES]


def gather_rows(rows, n, first, blocks, per):
    return jnp.concatenate(
        [rows[pl.ds(first + c, n, stride=blocks), :] for c in range(per)], axis=1
    )


def token_ranks(ids, experts):
    columns, tokens = ids.shape
    expert_at = lax.broadcasted_iota(jnp.int32, (experts, tokens), 0)
    matches = [ids[k : k + 1, :] == expert_at for k in range(columns)]
    named = jnp.zeros((experts, tokens), F32)
    for match in matches:
        named = named + match.astype(F32)
    row = lax.broadcasted_iota(jnp.int32, (tokens, tokens), 0)
    column = lax.broadcasted_iota(jnp.int32, (tokens, tokens), 1)
    earlier = (row < column).astype(F32).astype(BF16)
    return matches, named, dot(named.astype(BF16), earlier)


def identity(size):
    row = lax.broadcasted_iota(jnp.int32, (size, size), 0)
    column = lax.broadcasted_iota(jnp.int32, (size, size), 1)
    return (row == column).astype(F32).astype(BF16)


def prepare_kernel(tokens, cotangent, ids, weights, gate, up, down, out, packed, rows):
    features, hidden = gate.shape
    for i, weight in enumerate((gate, up)):
        for c in range(hidden // LANES):
            at = i * hidden + c * LANES
            packed[at : at + features, :] = weight[:, c * LANES : (c + 1) * LANES]
    packed[2 * hidden :, :] = down[...]
    per = tokens.shape[1] // LANES
    blocks = 2 * CAP * per
    experts = out.shape[0] // blocks
    matches, named, rank = token_ranks(ids[...], experts)
    scale = jnp.zeros(named.shape, F32)
    values = weights[...].astype(F32)
    for k, match in enumerate(matches):
        scale = scale + jnp.where(match, values[k : k + 1, :], 0.0)
    for r in range(CAP):
        here = (named > 0.0) & (rank == float(r))
        pick = jnp.where(here, 1.0, 0.0).astype(BF16)
        scaled = jnp.where(here, scale, 0.0).astype(BF16)
        spread_rows(dot(pick, tokens[...]), rows, r * per, blocks)
        spread_rows(dot(scaled, cotangent[...]), rows, (CAP + r) * per, blocks)
    out[...] = rows[...].astype(BF16)


def expert_kernel(place, recv, *refs):
    pieces, outs, scratch = refs[:9], refs[9:19], refs[19:]
    back, terms = outs[0], outs[1:]
    rows, gate_up, down, term, down_term, sems = scratch
    peers, features, _ = gate_up.shape
    hidden = down.shape[1]
    width = peers * features
    per = width // LANES
    blocks = 2 * CAP * per
    sources = recv.shape[0] // blocks
    me = place[0]
    tiles = 2 * hidden // LANES
    early, late = [], []
    starts = [0, -1, -2, -3, 1, 2, 3, 4, 4]
    for n, (piece, offset) in enumerate(zip(pieces, starts)):
        d = lax.rem(me + offset + peers, peers)
        first = pieces[7].shape[0] if n == 8 else 0
        for i in range(piece.shape[0] // LANES):
            at = first // LANES + i
            if at < tiles:
                target = gate_up.at[d, :, pl.ds(at * LANES, LANES)]
            else:
                target = down.at[d, pl.ds((at - tiles) * LANES, LANES), :]
            copy = pltpu.make_async_copy(
                piece.at[pl.ds(i * LANES, LANES), :], target, sems.at[n, i]
            )
            (early if at < tiles else late).append(copy)
    for copy in early + late:
        copy.start()
    rows[...] = recv[...].astype(F32)
    x = jnp.concatenate(
        [gather_rows(rows, sources, r * per, blocks, per).astype(BF16) for r in range(CAP)], axis=0
    )
    g = jnp.concatenate(
        [gather_rows(rows, sources, (CAP + r) * per, blocks, per).astype(BF16) for r in range(CAP)],
        axis=0,
    )
    for copy in early:
        copy.wait()
    wide = gate_up[...].reshape(width, 2 * hidden)
    pre = dot(x, wide)
    gate_pre, up_pre = pre[:, :hidden], pre[:, hidden:]
    sigmoid = 1.0 / (1.0 + jnp.exp(-gate_pre))
    inner = (gate_pre * sigmoid * up_pre).astype(BF16)
    for copy in late:
        copy.wait()
    narrow = jnp.concatenate([down[d] for d in range(peers)], axis=1)
    hidden_grad = dot(g, narrow, ((1,), (1,)))
    out = dot(inner, narrow)
    for r in range(CAP):
        spread_rows(out[r * sources : (r + 1) * sources], rows, r * per, blocks)
    gate_grad = (hidden_grad * up_pre * sigmoid * (1.0 + gate_pre * (1.0 - sigmoid))).astype(BF16)
    up_grad = (hidden_grad * gate_pre * sigmoid).astype(BF16)
    both = jnp.concatenate([gate_grad, up_grad], axis=1)
    back_grad = dot(both, wide, ((1,), (1,)))
    for r in range(CAP):
        spread_rows(back_grad[r * sources : (r + 1) * sources], rows, (CAP + r) * per, blocks)
    back[...] = rows[...].astype(BF16)
    term[...] = dot(x, both, ((0,), (0,))).astype(BF16).reshape(term.shape)
    down_full = dot(inner, g, ((0,), (0,))).astype(BF16)
    for d in range(peers):
        down_term[d] = down_full[:, d * features : (d + 1) * features]
    for n, (ref, offset) in enumerate(zip(terms, [0, 1, 2, 3, 5, 6, 7, 4, 4])):
        d = lax.rem(me + offset, peers)
        first = terms[7].shape[0] if n == 8 else 0
        for i in range(ref.shape[0] // LANES):
            at = first // LANES + i
            if at < tiles:
                ref[i * LANES : (i + 1) * LANES, :] = term[d, :, at * LANES : (at + 1) * LANES]
            else:
                ref[i * LANES : (i + 1) * LANES, :] = down_term[
                    d, (at - tiles) * LANES : (at - tiles + 1) * LANES, :
                ]


def combine_kernel(back, cotangent, ids, weights, layer, token_grads, router_grads, rows):
    tokens, width = cotangent.shape
    columns = ids.shape[0]
    per = width // LANES
    blocks = 2 * CAP * per
    experts = back.shape[0] // blocks
    rows[...] = back[...].astype(F32)
    matches, named, rank = token_ranks(ids[...], experts)
    ranks = [rank == float(r) for r in range(CAP)]
    pick = jnp.concatenate(
        [
            jnp.concatenate([jnp.where(match & at, 1.0, 0.0) for match in matches], axis=1)
            for at in ranks
        ],
        axis=0,
    ).astype(BF16)
    outs = jnp.concatenate(
        [gather_rows(rows, experts, r * per, blocks, per).astype(BF16) for r in range(CAP)], axis=0
    )
    grads = jnp.concatenate(
        [
            gather_rows(rows, experts, (CAP + r) * per, blocks, per).astype(BF16)
            for r in range(CAP)
        ],
        axis=0,
    )
    out = dot(pick, outs, ((0,), (0,)))
    grad = dot(pick, grads, ((0,), (0,)))
    eye = identity(tokens)
    values = dot(eye, weights[...], ((1,), (1,)))
    cot = cotangent[...].astype(F32)
    lane = lax.broadcasted_iota(jnp.int32, (tokens, columns), 1)
    total = jnp.zeros((tokens, width), F32)
    total_grad = jnp.zeros((tokens, width), F32)
    routed = jnp.zeros((tokens, columns), F32)
    for j in range(columns // 2):
        a, b = 2 * j, 2 * j + 1
        first, second = out[a * tokens : (a + 1) * tokens], out[b * tokens : (b + 1) * tokens]
        pair = values[:, a : a + 1] * first + values[:, b : b + 1] * second
        total = total + pair.astype(BF16).astype(F32)
        pair = grad[a * tokens : (a + 1) * tokens] + grad[b * tokens : (b + 1) * tokens]
        total_grad = total_grad + pair.astype(BF16).astype(F32)
        routed = jnp.where(lane == a, jnp.sum(cot * first, axis=1, keepdims=True), routed)
        routed = jnp.where(lane == b, jnp.sum(cot * second, axis=1, keepdims=True), routed)
    layer[...] = total.astype(BF16)
    token_grads[...] = total_grad.astype(BF16)
    router_grads[...] = dot(routed.astype(BF16), eye, ((0,), (0,))).astype(BF16)


def unpack_kernel(own, right, left, gate, up, down):
    features, hidden = gate.shape
    total = (own[...].astype(F32) + right[...].astype(F32) + left[...].astype(F32)).astype(BF16)
    for i, weight in enumerate((gate, up)):
        for c in range(hidden // LANES):
            at = i * hidden + c * LANES
            weight[:, c * LANES : (c + 1) * LANES] = total[at : at + features, :]
    down[...] = total[2 * hidden :, :]


def call(kernel, outs, scratch=(), in_specs=None, name=None):
    shapes = [jax.ShapeDtypeStruct(shape, BF16) for shape in outs]
    single = len(shapes) == 1
    return pl.pallas_call(
        kernel,
        out_shape=shapes[0] if single else shapes,
        in_specs=in_specs,
        out_specs=vmem() if single else [vmem() for _ in shapes],
        scratch_shapes=list(scratch),
        interpret=INTERPRET,
        name=name,
    )


def prepare(tokens, cotangent, ids, weights, gate, up, down, experts):
    lines = experts * 2 * CAP * tokens.shape[1] // LANES
    return call(
        prepare_kernel,
        [(lines, LANES), (3 * gate.shape[1], LANES)],
        scratch=[pltpu.VMEM((lines, LANES), F32)],
        in_specs=[vmem()] * 7,
        name="prepare",
    )(tokens, cotangent, ids, weights, gate, up, down)


def expert(place, recv, pieces, hidden, width):
    peers = width // LANES
    lines, half = pieces[0].shape[0], pieces[7].shape[0]
    first, second = half, lines - half
    shapes = [(lines, LANES)] * 7 + [(first, LANES), (second, LANES)]
    return call(
        expert_kernel,
        [recv.shape] + shapes,
        scratch=[
            pltpu.VMEM(recv.shape, F32),
            pltpu.VMEM((peers, LANES, 2 * hidden), BF16),
            pltpu.VMEM((peers, hidden, LANES), BF16),
            pltpu.VMEM((peers, LANES, 2 * hidden), BF16),
            pltpu.VMEM((peers, hidden, LANES), BF16),
            pltpu.SemaphoreType.DMA((9, lines // LANES)),
        ],
        in_specs=[pl.BlockSpec(memory_space=pltpu.SMEM), vmem()]
        + [pl.BlockSpec(memory_space=pl.ANY)] * 9,
        name="expert",
    )(place, recv, *pieces)


def shifted(value, by):
    peers = lax.axis_size("dp")
    return lax.ppermute(value, "dp", [(i, (i + by) % peers) for i in range(peers)])


def gather_ring(chunk):
    half = far_half(chunk.shape[0])
    right, left = [chunk], [chunk]
    for _ in range(3):
        right.append(shifted(right[-1], 1))
        left.append(shifted(left[-1], -1))
    far = [shifted(right[-1][:half], 1), shifted(left[-1][half:], -1)]
    return right + left[1:] + far


def far_half(lines):
    return lines // LANES // 2 * LANES + lines // LANES % 2 * LANES


def scatter_ring(terms):
    own, near, two, three, far3, far2, far1, first, second = terms
    half = first.shape[0]
    right, left = shifted(first, 1), shifted(second, -1)
    right = jnp.concatenate([three[:half] + right, three[half:]], axis=0)
    left = jnp.concatenate([far3[:half], far3[half:] + left], axis=0)
    right, left = shifted(right, 1), shifted(left, -1)
    right, left = shifted(two + right, 1), shifted(far2 + left, -1)
    right, left = shifted(near + right, 1), shifted(far1 + left, -1)
    return own, right, left


def combine(back, cotangent, ids, weights):
    return call(
        combine_kernel,
        [cotangent.shape, cotangent.shape, ids.shape],
        scratch=[pltpu.VMEM(back.shape, F32)],
        in_specs=[vmem()] * 4,
        name="combine",
    )(back, cotangent, ids, weights)


def unpack_grads(parts, features, hidden):
    return call(
        unpack_kernel,
        [(features, hidden), (features, hidden), (hidden, LANES)],
        in_specs=[vmem()] * 3,
        name="unpack_grads",
    )(*parts)


def exchange(lines, peers):
    out = lax.all_to_all(
        lines.reshape(peers, -1, LANES), ("group", "local"), split_axis=0, concat_axis=0, tiled=True
    )
    return out.reshape(lines.shape)


def local(tokens, cotangent, expert_ids, router_weights, gate_weight, up_weight, down_weight):
    experts = lax.axis_size("group") * lax.axis_size("local")
    features, hidden = gate_weight.shape[1:]
    width = tokens.shape[1]
    ids, weights = expert_ids.T, router_weights.T
    sent, packed = prepare(
        tokens, cotangent, ids, weights, gate_weight[0], up_weight[0], down_weight[0], experts
    )
    recv = exchange(sent, experts)
    pieces = gather_ring(packed)
    place = lax.axis_index("dp").astype(jnp.int32).reshape(1)
    back, *terms = expert(place, recv, pieces, hidden, width)
    returned = exchange(back, experts)
    parts = scatter_ring(terms)
    layer, token_grads, router_grads = combine(returned, cotangent, ids, weights)
    gate, up, down = unpack_grads(parts, features, hidden)
    return layer, token_grads, router_grads.T, gate[None], up[None], down[None]


def solution(mesh):
    tokens = P(("dp", "group", "local"), None)
    rows = P(("group", "local"), "dp", None)
    columns = P(("group", "local"), None, "dp")
    return jax.shard_map(
        local,
        mesh=mesh,
        in_specs=(tokens, tokens, tokens, tokens, rows, rows, columns),
        out_specs=(tokens, tokens, tokens, rows, rows, columns),
        check_vma=False,
    )
```

```python
import jax
import jax.numpy as jnp
from jax import lax
from jax.experimental import pallas as pl
from jax.experimental.pallas import tpu as pltpu
from jax.sharding import PartitionSpec as P


INTERPRET = False
BF16 = jnp.bfloat16
F32 = jnp.float32
LANES = 128
RING = (0, 7, 6, 5, 4, 1, 2, 3)
CAP = 3


def vmem():
    return pl.BlockSpec(memory_space=pltpu.VMEM)


def dot(a, b, dims=((1,), (0,))):
    return lax.dot_general(a, b, (dims, ((), ())), preferred_element_type=F32)


def spread_rows(wide, rows, first, blocks):
    n, features = wide.shape
    per = features // LANES
    for c in range(per):
        rows[pl.ds(first + c, n, stride=blocks), :] = wide[:, c * LANES : (c + 1) * LANES]


def gather_rows(rows, n, first, blocks, per):
    return jnp.concatenate(
        [rows[pl.ds(first + c, n, stride=blocks), :] for c in range(per)], axis=1
    )


def token_ranks(ids, experts):
    columns, tokens = ids.shape
    expert_at = lax.broadcasted_iota(jnp.int32, (experts, tokens), 0)
    matches = [ids[k : k + 1, :] == expert_at for k in range(columns)]
    named = jnp.zeros((experts, tokens), F32)
    for match in matches:
        named = named + match.astype(F32)
    row = lax.broadcasted_iota(jnp.int32, (tokens, tokens), 0)
    column = lax.broadcasted_iota(jnp.int32, (tokens, tokens), 1)
    earlier = (row < column).astype(F32).astype(BF16)
    return matches, named, dot(named.astype(BF16), earlier)


def identity(size):
    row = lax.broadcasted_iota(jnp.int32, (size, size), 0)
    column = lax.broadcasted_iota(jnp.int32, (size, size), 1)
    return (row == column).astype(F32).astype(BF16)


def prepare_kernel(tokens, cotangent, ids, weights, gate, up, down, out, packed, rows):
    features, hidden = gate.shape
    for i, weight in enumerate((gate, up)):
        for c in range(hidden // LANES):
            at = i * hidden + c * LANES
            packed[at : at + features, :] = weight[:, c * LANES : (c + 1) * LANES]
    packed[2 * hidden :, :] = down[...]
    per = tokens.shape[1] // LANES
    blocks = 2 * CAP * per
    experts = out.shape[0] // blocks
    matches, named, rank = token_ranks(ids[...], experts)
    scale = jnp.zeros(named.shape, F32)
    values = weights[...].astype(F32)
    for k, match in enumerate(matches):
        scale = scale + jnp.where(match, values[k : k + 1, :], 0.0)
    for r in range(CAP):
        here = (named > 0.0) & (rank == float(r))
        pick = jnp.where(here, 1.0, 0.0).astype(BF16)
        scaled = jnp.where(here, scale, 0.0).astype(BF16)
        spread_rows(dot(pick, tokens[...]), rows, r * per, blocks)
        spread_rows(dot(scaled, cotangent[...]), rows, (CAP + r) * per, blocks)
    out[...] = rows[...].astype(BF16)


def expert_kernel(place, recv, *refs):
    pieces, outs, scratch = refs[:8], refs[8:17], refs[17:]
    back, terms = outs[0], outs[1:]
    rows, gate_up, down, term, down_term, leaving, in_sems, out_sems, back_sem = scratch
    peers, features, _ = gate_up.shape
    hidden = down.shape[1]
    width = peers * features
    per = width // LANES
    blocks = 2 * CAP * per
    sources = recv.shape[0] // blocks
    me = place[0]
    tiles = 2 * hidden // LANES
    early, late = [], []
    for n, (piece, offset) in enumerate(zip(pieces, RING)):
        d = lax.rem(me + offset, peers)
        for i in range(tiles):
            early.append(
                pltpu.make_async_copy(
                    piece.at[pl.ds(i * LANES, LANES), :],
                    gate_up.at[d, :, pl.ds(i * LANES, LANES)],
                    in_sems.at[n, i],
                )
            )
        late.append(
            pltpu.make_async_copy(
                piece.at[pl.ds(2 * hidden, hidden), :], down.at[d], in_sems.at[n, tiles]
            )
        )
    for copy in early + late:
        copy.start()
    rows[...] = recv[...].astype(F32)
    x = jnp.concatenate(
        [gather_rows(rows, sources, r * per, blocks, per).astype(BF16) for r in range(CAP)], axis=0
    )
    g = jnp.concatenate(
        [gather_rows(rows, sources, (CAP + r) * per, blocks, per).astype(BF16) for r in range(CAP)],
        axis=0,
    )
    for copy in early:
        copy.wait()
    wide = gate_up[...].reshape(width, 2 * hidden)
    pre = dot(x, wide)
    gate_pre, up_pre = pre[:, :hidden], pre[:, hidden:]
    sigmoid = 1.0 / (1.0 + jnp.exp(-gate_pre))
    inner = (gate_pre * sigmoid * up_pre).astype(BF16)
    for copy in late:
        copy.wait()
    narrow = jnp.concatenate([down[d] for d in range(peers)], axis=1)
    hidden_grad = dot(g, narrow, ((1,), (1,)))
    out = dot(inner, narrow)
    for r in range(CAP):
        spread_rows(out[r * sources : (r + 1) * sources], rows, r * per, blocks)
    gate_grad = (hidden_grad * up_pre * sigmoid * (1.0 + gate_pre * (1.0 - sigmoid))).astype(BF16)
    up_grad = (hidden_grad * gate_pre * sigmoid).astype(BF16)
    both = jnp.concatenate([gate_grad, up_grad], axis=1)
    back_grad = dot(both, wide, ((1,), (1,)))
    for r in range(CAP):
        spread_rows(back_grad[r * sources : (r + 1) * sources], rows, (CAP + r) * per, blocks)
    leaving[...] = rows[...].astype(BF16)
    send_back = pltpu.make_async_copy(leaving, back, back_sem.at[0])
    send_back.start()
    down_full = dot(inner, g, ((0,), (0,))).astype(BF16)
    for d in range(peers):
        down_term[d] = down_full[:, d * features : (d + 1) * features]
    places = [lax.rem(me + offset, peers) for offset in range(peers)]
    copies = [
        pltpu.make_async_copy(
            down_term.at[d], ref.at[pl.ds(2 * hidden, hidden), :], out_sems.at[n, tiles]
        )
        for n, (ref, d) in enumerate(zip(terms, places))
    ]
    for copy in copies:
        copy.start()
    term[...] = dot(x, both, ((0,), (0,))).astype(BF16).reshape(term.shape)
    lines = [
        pltpu.make_async_copy(
            term.at[d, :, pl.ds(i * LANES, LANES)],
            ref.at[pl.ds(i * LANES, LANES), :],
            out_sems.at[n, i],
        )
        for n, (ref, d) in enumerate(zip(terms, places))
        for i in range(tiles)
    ]
    for copy in lines:
        copy.start()
    for copy in copies + lines:
        copy.wait()
    send_back.wait()


def combine_kernel(back, cotangent, ids, weights, layer, token_grads, router_grads, rows):
    tokens, width = cotangent.shape
    columns = ids.shape[0]
    per = width // LANES
    blocks = 2 * CAP * per
    experts = back.shape[0] // blocks
    rows[...] = back[...].astype(F32)
    matches, _, rank = token_ranks(ids[...], experts)
    ranks = [rank == float(r) for r in range(CAP)]
    pick = jnp.concatenate(
        [
            jnp.concatenate([jnp.where(match & at, 1.0, 0.0) for match in matches], axis=1)
            for at in ranks
        ],
        axis=0,
    ).astype(BF16)
    outs = jnp.concatenate(
        [gather_rows(rows, experts, r * per, blocks, per).astype(BF16) for r in range(CAP)], axis=0
    )
    grads = jnp.concatenate(
        [
            gather_rows(rows, experts, (CAP + r) * per, blocks, per).astype(BF16)
            for r in range(CAP)
        ],
        axis=0,
    )
    out = dot(pick, outs, ((0,), (0,)))
    grad = dot(pick, grads, ((0,), (0,)))
    eye = identity(tokens)
    values = dot(eye, weights[...], ((1,), (1,)))
    cot = cotangent[...].astype(F32)
    lane = lax.broadcasted_iota(jnp.int32, (tokens, columns), 1)
    total = jnp.zeros((tokens, width), F32)
    total_grad = jnp.zeros((tokens, width), F32)
    routed = jnp.zeros((tokens, columns), F32)
    for j in range(columns // 2):
        a, b = 2 * j, 2 * j + 1
        first, second = out[a * tokens : (a + 1) * tokens], out[b * tokens : (b + 1) * tokens]
        pair = values[:, a : a + 1] * first + values[:, b : b + 1] * second
        total = total + pair.astype(BF16).astype(F32)
        pair = grad[a * tokens : (a + 1) * tokens] + grad[b * tokens : (b + 1) * tokens]
        total_grad = total_grad + pair.astype(BF16).astype(F32)
        routed = jnp.where(lane == a, jnp.sum(cot * first, axis=1, keepdims=True), routed)
        routed = jnp.where(lane == b, jnp.sum(cot * second, axis=1, keepdims=True), routed)
    layer[...] = total.astype(BF16)
    token_grads[...] = total_grad.astype(BF16)
    router_grads[...] = dot(routed.astype(BF16), eye, ((0,), (0,))).astype(BF16)


def unpack_kernel(own, right, left, gate, up, down):
    features, hidden = gate.shape
    total = (own[...].astype(F32) + right[...].astype(F32) + left[...].astype(F32)).astype(BF16)
    for i, weight in enumerate((gate, up)):
        for c in range(hidden // LANES):
            at = i * hidden + c * LANES
            weight[:, c * LANES : (c + 1) * LANES] = total[at : at + features, :]
    down[...] = total[2 * hidden :, :]


def call(kernel, outs, scratch=(), in_specs=None):
    shapes = [jax.ShapeDtypeStruct(shape, BF16) for shape in outs]
    single = len(shapes) == 1
    return pl.pallas_call(
        kernel,
        out_shape=shapes[0] if single else shapes,
        in_specs=in_specs,
        out_specs=vmem() if single else [vmem() for _ in shapes],
        scratch_shapes=list(scratch),
        interpret=INTERPRET,
    )


def prepare(tokens, cotangent, ids, weights, gate, up, down, experts):
    lines = experts * 2 * CAP * tokens.shape[1] // LANES
    return call(
        prepare_kernel,
        [(lines, LANES), (3 * gate.shape[1], LANES)],
        scratch=[pltpu.VMEM((lines, LANES), F32)],
        in_specs=[vmem()] * 7,
    )(tokens, cotangent, ids, weights, gate, up, down)


def expert(place, recv, pieces, hidden, width):
    peers = width // LANES
    lines = pieces[0].shape[0]
    anywhere = pl.BlockSpec(memory_space=pl.ANY)
    copies = 2 * hidden // LANES + 1
    return pl.pallas_call(
        expert_kernel,
        out_shape=[jax.ShapeDtypeStruct(recv.shape, BF16)]
        + [jax.ShapeDtypeStruct((lines, LANES), BF16)] * peers,
        in_specs=[pl.BlockSpec(memory_space=pltpu.SMEM), vmem()] + [anywhere] * peers,
        out_specs=[anywhere] * (1 + peers),
        scratch_shapes=[
            pltpu.VMEM(recv.shape, F32),
            pltpu.VMEM((peers, LANES, 2 * hidden), BF16),
            pltpu.VMEM((peers, hidden, LANES), BF16),
            pltpu.VMEM((peers, LANES, 2 * hidden), BF16),
            pltpu.VMEM((peers, hidden, LANES), BF16),
            pltpu.VMEM(recv.shape, BF16),
            pltpu.SemaphoreType.DMA((peers, copies)),
            pltpu.SemaphoreType.DMA((peers, copies)),
            pltpu.SemaphoreType.DMA((1,)),
        ],
        interpret=INTERPRET,
        name="expert",
    )(place, recv, *pieces)


def shifted(value, by):
    peers = lax.axis_size("dp")
    return lax.ppermute(value, "dp", [(i, (i + by) % peers) for i in range(peers)])


def gather_ring(chunk):
    right, left = [chunk], [chunk]
    for _ in range(4):
        right.append(shifted(right[-1], 1))
    for _ in range(3):
        left.append(shifted(left[-1], -1))
    return right + left[1:]


def scatter_ring(terms):
    right = shifted(terms[4], 1)
    left = shifted(terms[5], -1)
    for step in (1, 2, 3):
        right = shifted(terms[4 - step] + right, 1)
        if step < 3:
            left = shifted(terms[5 + step] + left, -1)
    return terms[0], right, left


def combine(back, cotangent, ids, weights):
    return call(
        combine_kernel,
        [cotangent.shape, cotangent.shape, ids.shape],
        scratch=[pltpu.VMEM(back.shape, F32)],
        in_specs=[vmem()] * 4,
    )(back, cotangent, ids, weights)


def unpack_grads(parts, features, hidden):
    return call(
        unpack_kernel,
        [(features, hidden), (features, hidden), (hidden, LANES)],
        in_specs=[vmem()] * 3,
    )(*parts)


def exchange(lines, peers):
    out = lax.all_to_all(
        lines.reshape(peers, -1, LANES),
        ("group", "local"),
        split_axis=0,
        concat_axis=0,
        tiled=True,
    )
    return out.reshape(lines.shape)


def local(tokens, cotangent, expert_ids, router_weights, gate_weight, up_weight, down_weight):
    experts = lax.axis_size("group") * lax.axis_size("local")
    features, hidden = gate_weight.shape[1:]
    width = tokens.shape[1]
    ids, weights = expert_ids.T, router_weights.T
    sent, packed = prepare(
        tokens, cotangent, ids, weights, gate_weight[0], up_weight[0], down_weight[0], experts
    )
    recv = exchange(sent, experts)
    pieces = gather_ring(packed)
    place = lax.axis_index("dp").astype(jnp.int32).reshape(1)
    back, *terms = expert(place, recv, pieces, hidden, width)
    returned = exchange(back, experts)
    parts = scatter_ring(terms)
    layer, token_grads, router_grads = combine(returned, cotangent, ids, weights)
    gate, up, down = unpack_grads(parts, features, hidden)
    return layer, token_grads, router_grads.T, gate[None], up[None], down[None]


def solution(mesh):
    tokens = P(("dp", "group", "local"), None)
    rows = P(("group", "local"), "dp", None)
    columns = P(("group", "local"), None, "dp")
    return jax.shard_map(
        local,
        mesh=mesh,
        in_specs=(tokens, tokens, tokens, tokens, rows, rows, columns),
        out_specs=(tokens, tokens, tokens, rows, rows, columns),
        check_vma=False,
    )
```

```python
import jax
import jax.numpy as jnp
from jax import lax
from jax.experimental import pallas as pl
from jax.experimental.pallas import tpu as pltpu
from jax.sharding import PartitionSpec as P


INTERPRET = False
BF16 = jnp.bfloat16
F32 = jnp.float32
LANES = 128
RING = (0, 7, 6, 5, 4, 1, 2, 3)
CAP = 3


def vmem():
    return pl.BlockSpec(memory_space=pltpu.VMEM)


def dot(a, b, dims=((1,), (0,))):
    return lax.dot_general(a, b, (dims, ((), ())), preferred_element_type=F32)


def spread_rows(wide, rows, first, blocks):
    n, features = wide.shape
    per = features // LANES
    for c in range(per):
        rows[pl.ds(first + c, n, stride=blocks), :] = wide[:, c * LANES : (c + 1) * LANES]


def gather_rows(rows, n, first, blocks, per):
    return jnp.concatenate(
        [rows[pl.ds(first + c, n, stride=blocks), :] for c in range(per)], axis=1
    )


def token_ranks(ids, experts):
    columns, tokens = ids.shape
    expert_at = lax.broadcasted_iota(jnp.int32, (experts, tokens), 0)
    matches = [ids[k : k + 1, :] == expert_at for k in range(columns)]
    named = jnp.zeros((experts, tokens), F32)
    for match in matches:
        named = named + match.astype(F32)
    row = lax.broadcasted_iota(jnp.int32, (tokens, tokens), 0)
    column = lax.broadcasted_iota(jnp.int32, (tokens, tokens), 1)
    earlier = (row < column).astype(F32).astype(BF16)
    return matches, named, dot(named.astype(BF16), earlier)


def identity(size):
    row = lax.broadcasted_iota(jnp.int32, (size, size), 0)
    column = lax.broadcasted_iota(jnp.int32, (size, size), 1)
    return (row == column).astype(F32).astype(BF16)


def prepare_kernel(tokens, cotangent, ids, weights, gate, up, down, out, packed, rows):
    features, hidden = gate.shape
    for i, weight in enumerate((gate, up)):
        for c in range(hidden // LANES):
            at = i * hidden + c * LANES
            packed[at : at + features, :] = weight[:, c * LANES : (c + 1) * LANES]
    packed[2 * hidden :, :] = down[...]
    per = tokens.shape[1] // LANES
    blocks = 2 * CAP * per
    experts = out.shape[0] // blocks
    matches, named, rank = token_ranks(ids[...], experts)
    scale = jnp.zeros(named.shape, F32)
    values = weights[...].astype(F32)
    for k, match in enumerate(matches):
        scale = scale + jnp.where(match, values[k : k + 1, :], 0.0)
    for r in range(CAP):
        here = (named > 0.0) & (rank == float(r))
        pick = jnp.where(here, 1.0, 0.0).astype(BF16)
        scaled = jnp.where(here, scale, 0.0).astype(BF16)
        spread_rows(dot(pick, tokens[...]), rows, r * per, blocks)
        spread_rows(dot(scaled, cotangent[...]), rows, (CAP + r) * per, blocks)
    out[...] = rows[...].astype(BF16)


def expert_kernel(place, recv, *refs):
    pieces, outs, scratch = refs[:8], refs[8:17], refs[17:]
    back, terms = outs[0], outs[1:]
    rows, gate_up, down, term, down_term, leaving, in_sems, out_sems, back_sem = scratch
    peers, features, _ = gate_up.shape
    hidden = down.shape[1]
    width = peers * features
    per = width // LANES
    blocks = 2 * CAP * per
    sources = recv.shape[0] // blocks
    me = place[0]
    tiles = 2 * hidden // LANES
    early, late = [], []
    for n, (piece, offset) in enumerate(zip(pieces, RING)):
        d = lax.rem(me + offset, peers)
        for i in range(tiles):
            early.append(
                pltpu.make_async_copy(
                    piece.at[pl.ds(i * LANES, LANES), :],
                    gate_up.at[d, :, pl.ds(i * LANES, LANES)],
                    in_sems.at[n, i],
                )
            )
        late.append(
            pltpu.make_async_copy(
                piece.at[pl.ds(2 * hidden, hidden), :], down.at[d], in_sems.at[n, tiles]
            )
        )
    for copy in early + late:
        copy.start()
    rows[...] = recv[...].astype(F32)
    x = jnp.concatenate(
        [gather_rows(rows, sources, r * per, blocks, per).astype(BF16) for r in range(CAP)], axis=0
    )
    g = jnp.concatenate(
        [gather_rows(rows, sources, (CAP + r) * per, blocks, per).astype(BF16) for r in range(CAP)],
        axis=0,
    )
    for copy in early:
        copy.wait()
    wide = gate_up[...].reshape(width, 2 * hidden)
    pre = dot(x, wide)
    gate_pre, up_pre = pre[:, :hidden], pre[:, hidden:]
    sigmoid = 1.0 / (1.0 + jnp.exp(-gate_pre))
    inner = (gate_pre * sigmoid * up_pre).astype(BF16)
    for copy in late:
        copy.wait()
    narrow = jnp.concatenate([down[d] for d in range(peers)], axis=1)
    hidden_grad = dot(g, narrow, ((1,), (1,)))
    out = dot(inner, narrow)
    for r in range(CAP):
        spread_rows(out[r * sources : (r + 1) * sources], rows, r * per, blocks)
    gate_grad = (hidden_grad * up_pre * sigmoid * (1.0 + gate_pre * (1.0 - sigmoid))).astype(BF16)
    up_grad = (hidden_grad * gate_pre * sigmoid).astype(BF16)
    both = jnp.concatenate([gate_grad, up_grad], axis=1)
    back_grad = dot(both, wide, ((1,), (1,)))
    for r in range(CAP):
        spread_rows(back_grad[r * sources : (r + 1) * sources], rows, (CAP + r) * per, blocks)
    leaving[...] = rows[...].astype(BF16)
    send_back = pltpu.make_async_copy(leaving, back, back_sem.at[0])
    send_back.start()
    down_full = dot(inner, g, ((0,), (0,))).astype(BF16)
    for d in range(peers):
        down_term[d] = down_full[:, d * features : (d + 1) * features]
    places = [lax.rem(me + offset, peers) for offset in range(peers)]
    copies = [
        pltpu.make_async_copy(
            down_term.at[d], ref.at[pl.ds(2 * hidden, hidden), :], out_sems.at[n, tiles]
        )
        for n, (ref, d) in enumerate(zip(terms, places))
    ]
    for copy in copies:
        copy.start()
    term[...] = dot(x, both, ((0,), (0,))).astype(BF16).reshape(term.shape)
    lines = [
        pltpu.make_async_copy(
            term.at[d, :, pl.ds(i * LANES, LANES)],
            ref.at[pl.ds(i * LANES, LANES), :],
            out_sems.at[n, i],
        )
        for n, (ref, d) in enumerate(zip(terms, places))
        for i in range(tiles)
    ]
    for copy in lines:
        copy.start()
    for copy in copies + lines:
        copy.wait()
    send_back.wait()


def combine_kernel(back, cotangent, ids, weights, layer, token_grads, router_grads, rows):
    tokens, width = cotangent.shape
    columns = ids.shape[0]
    per = width // LANES
    blocks = 2 * CAP * per
    experts = back.shape[0] // blocks
    rows[...] = back[...].astype(F32)
    matches, _, rank = token_ranks(ids[...], experts)
    ranks = [rank == float(r) for r in range(CAP)]
    pick = jnp.concatenate(
        [
            jnp.concatenate([jnp.where(match & at, 1.0, 0.0) for match in matches], axis=1)
            for at in ranks
        ],
        axis=0,
    ).astype(BF16)
    outs = jnp.concatenate(
        [gather_rows(rows, experts, r * per, blocks, per).astype(BF16) for r in range(CAP)], axis=0
    )
    grads = jnp.concatenate(
        [
            gather_rows(rows, experts, (CAP + r) * per, blocks, per).astype(BF16)
            for r in range(CAP)
        ],
        axis=0,
    )
    out = dot(pick, outs, ((0,), (0,)))
    grad = dot(pick, grads, ((0,), (0,)))
    eye = identity(tokens)
    values = dot(eye, weights[...], ((1,), (1,)))
    cot = cotangent[...].astype(F32)
    lane = lax.broadcasted_iota(jnp.int32, (tokens, columns), 1)
    total = jnp.zeros((tokens, width), F32)
    total_grad = jnp.zeros((tokens, width), F32)
    routed = jnp.zeros((tokens, columns), F32)
    for j in range(columns // 2):
        a, b = 2 * j, 2 * j + 1
        first, second = out[a * tokens : (a + 1) * tokens], out[b * tokens : (b + 1) * tokens]
        pair = values[:, a : a + 1] * first + values[:, b : b + 1] * second
        total = total + pair.astype(BF16).astype(F32)
        pair = grad[a * tokens : (a + 1) * tokens] + grad[b * tokens : (b + 1) * tokens]
        total_grad = total_grad + pair.astype(BF16).astype(F32)
        routed = jnp.where(lane == a, jnp.sum(cot * first, axis=1, keepdims=True), routed)
        routed = jnp.where(lane == b, jnp.sum(cot * second, axis=1, keepdims=True), routed)
    layer[...] = total.astype(BF16)
    token_grads[...] = total_grad.astype(BF16)
    router_grads[...] = dot(routed.astype(BF16), eye, ((0,), (0,))).astype(BF16)


def finish_kernel(back, own, right, left, cotangent, ids, weights, *refs):
    layer, token_grads, router_grads, gate, up, down, lines, rows, sems = refs
    copies = [
        pltpu.make_async_copy(part, lines.at[i], sems.at[i])
        for i, part in enumerate((own, right, left))
    ]
    for copy in copies:
        copy.start()
    combine_kernel(back, cotangent, ids, weights, layer, token_grads, router_grads, rows)
    for copy in copies:
        copy.wait()
    features, hidden = gate.shape
    total = (
        lines[0].astype(F32) + lines[1].astype(F32) + lines[2].astype(F32)
    ).astype(BF16)
    for i, weight in enumerate((gate, up)):
        for c in range(hidden // LANES):
            at = i * hidden + c * LANES
            weight[:, c * LANES : (c + 1) * LANES] = total[at : at + features, :]
    down[...] = total[2 * hidden :, :]


def call(kernel, outs, scratch=(), in_specs=None):
    shapes = [jax.ShapeDtypeStruct(shape, BF16) for shape in outs]
    single = len(shapes) == 1
    return pl.pallas_call(
        kernel,
        out_shape=shapes[0] if single else shapes,
        in_specs=in_specs,
        out_specs=vmem() if single else [vmem() for _ in shapes],
        scratch_shapes=list(scratch),
        interpret=INTERPRET,
    )


def prepare(tokens, cotangent, ids, weights, gate, up, down, experts):
    lines = experts * 2 * CAP * tokens.shape[1] // LANES
    return call(
        prepare_kernel,
        [(lines, LANES), (3 * gate.shape[1], LANES)],
        scratch=[pltpu.VMEM((lines, LANES), F32)],
        in_specs=[vmem()] * 7,
    )(tokens, cotangent, ids, weights, gate, up, down)


def expert(place, recv, pieces, hidden, width):
    peers = width // LANES
    lines = pieces[0].shape[0]
    anywhere = pl.BlockSpec(memory_space=pl.ANY)
    copies = 2 * hidden // LANES + 1
    return pl.pallas_call(
        expert_kernel,
        out_shape=[jax.ShapeDtypeStruct(recv.shape, BF16)]
        + [jax.ShapeDtypeStruct((lines, LANES), BF16)] * peers,
        in_specs=[pl.BlockSpec(memory_space=pltpu.SMEM), vmem()] + [anywhere] * peers,
        out_specs=[anywhere] * (1 + peers),
        scratch_shapes=[
            pltpu.VMEM(recv.shape, F32),
            pltpu.VMEM((peers, LANES, 2 * hidden), BF16),
            pltpu.VMEM((peers, hidden, LANES), BF16),
            pltpu.VMEM((peers, LANES, 2 * hidden), BF16),
            pltpu.VMEM((peers, hidden, LANES), BF16),
            pltpu.VMEM(recv.shape, BF16),
            pltpu.SemaphoreType.DMA((peers, copies)),
            pltpu.SemaphoreType.DMA((peers, copies)),
            pltpu.SemaphoreType.DMA((1,)),
        ],
        interpret=INTERPRET,
        name="expert",
    )(place, recv, *pieces)


def shifted(value, by):
    peers = lax.axis_size("dp")
    return lax.ppermute(value, "dp", [(i, (i + by) % peers) for i in range(peers)])


def gather_ring(chunk):
    right, left = [chunk], [chunk]
    for _ in range(4):
        right.append(shifted(right[-1], 1))
    for _ in range(3):
        left.append(shifted(left[-1], -1))
    return right + left[1:]


def scatter_ring(terms):
    right = shifted(terms[4], 1)
    left = shifted(terms[5], -1)
    for step in (1, 2, 3):
        right = shifted(terms[4 - step] + right, 1)
        if step < 3:
            left = shifted(terms[5 + step] + left, -1)
    return terms[0], right, left


def finish(back, cotangent, ids, weights, parts, features, hidden):
    anywhere = pl.BlockSpec(memory_space=pl.ANY)
    return call(
        finish_kernel,
        [
            cotangent.shape,
            cotangent.shape,
            ids.shape,
            (features, hidden),
            (features, hidden),
            (hidden, LANES),
        ],
        scratch=[
            pltpu.VMEM((3,) + parts[0].shape, BF16),
            pltpu.VMEM(back.shape, F32),
            pltpu.SemaphoreType.DMA((3,)),
        ],
        in_specs=[vmem()] + [anywhere] * 3 + [vmem()] * 3,
    )(back, *parts, cotangent, ids, weights)


def on_chip(value):
    return value if INTERPRET else pltpu.with_memory_space_constraint(value, pltpu.VMEM)


def exchange(lines, peers):
    out = lax.all_to_all(
        lines.reshape(peers, -1, LANES),
        ("group", "local"),
        split_axis=0,
        concat_axis=0,
        tiled=True,
    )
    return out.reshape(lines.shape)


def local(tokens, cotangent, expert_ids, router_weights, gate_weight, up_weight, down_weight):
    experts = lax.axis_size("group") * lax.axis_size("local")
    features, hidden = gate_weight.shape[1:]
    width = tokens.shape[1]
    ids, weights = expert_ids.T, router_weights.T
    sent, packed = prepare(
        tokens, cotangent, ids, weights, gate_weight[0], up_weight[0], down_weight[0], experts
    )
    recv = exchange(sent, experts)
    pieces = gather_ring(packed)
    place = lax.axis_index("dp").astype(jnp.int32).reshape(1)
    back, *terms = expert(place, on_chip(recv), pieces, hidden, width)
    returned = exchange(back, experts)
    parts = scatter_ring(terms)
    layer, token_grads, router_grads, gate, up, down = finish(
        on_chip(returned), cotangent, ids, weights, parts, features, hidden
    )
    return layer, token_grads, router_grads.T, gate[None], up[None], down[None]


def solution(mesh):
    tokens = P(("dp", "group", "local"), None)
    rows = P(("group", "local"), "dp", None)
    columns = P(("group", "local"), None, "dp")
    return jax.shard_map(
        local,
        mesh=mesh,
        in_specs=(tokens, tokens, tokens, tokens, rows, rows, columns),
        out_specs=(tokens, tokens, tokens, rows, rows, columns),
        check_vma=False,
    )
```

```python
import jax
import jax.numpy as jnp
from jax import lax
from jax.experimental import pallas as pl
from jax.experimental.pallas import tpu as pltpu
from jax.sharding import PartitionSpec as P


INTERPRET = False
BF16 = jnp.bfloat16
F32 = jnp.float32
LANES = 128
RING = (0, 7, 6, 5, 4, 1, 2, 3)
CAP = 3


def vmem():
    return pl.BlockSpec(memory_space=pltpu.VMEM)


def dot(a, b, dims=((1,), (0,))):
    return lax.dot_general(a, b, (dims, ((), ())), preferred_element_type=F32)


def spread_rows(wide, rows, first, blocks):
    n, features = wide.shape
    per = features // LANES
    for c in range(per):
        rows[pl.ds(first + c, n, stride=blocks), :] = wide[:, c * LANES : (c + 1) * LANES]


def gather_rows(rows, n, first, blocks, per):
    return jnp.concatenate(
        [rows[pl.ds(first + c, n, stride=blocks), :] for c in range(per)], axis=1
    )


def token_ranks(ids, experts):
    columns, tokens = ids.shape
    expert_at = lax.broadcasted_iota(jnp.int32, (experts, tokens), 0)
    matches = [ids[k : k + 1, :] == expert_at for k in range(columns)]
    named = jnp.zeros((experts, tokens), F32)
    for match in matches:
        named = named + match.astype(F32)
    row = lax.broadcasted_iota(jnp.int32, (tokens, tokens), 0)
    column = lax.broadcasted_iota(jnp.int32, (tokens, tokens), 1)
    earlier = (row < column).astype(F32).astype(BF16)
    return matches, named, dot(named.astype(BF16), earlier)


def prepare_kernel(tokens, cotangent, ids, weights, gate, up, down, out, packed, rows):
    features, hidden = gate.shape
    for i, weight in enumerate((gate, up)):
        for c in range(hidden // LANES):
            at = i * hidden + c * LANES
            packed[at : at + features, :] = weight[:, c * LANES : (c + 1) * LANES]
    packed[2 * hidden :, :] = down[...]
    per = tokens.shape[1] // LANES
    blocks = 2 * CAP * per
    experts = out.shape[0] // blocks
    matches, named, rank = token_ranks(ids[...], experts)
    scale = jnp.zeros(named.shape, F32)
    values = weights[...].astype(F32)
    for k, match in enumerate(matches):
        scale = scale + jnp.where(match, values[k : k + 1, :], 0.0)
    for r in range(CAP):
        here = (named > 0.0) & (rank == float(r))
        pick = jnp.where(here, 1.0, 0.0).astype(BF16)
        scaled = jnp.where(here, scale, 0.0).astype(BF16)
        spread_rows(dot(pick, tokens[...]), rows, r * per, blocks)
        spread_rows(dot(scaled, cotangent[...]), rows, (CAP + r) * per, blocks)
    out[...] = rows[...].astype(BF16)


def expert_kernel(place, recv, *refs):
    pieces, outs, scratch = refs[:8], refs[8:17], refs[17:]
    back, terms = outs[0], outs[1:]
    rows, gate_up, down, term, down_term, leaving, in_sems, out_sems, back_sem = scratch
    peers, features, _ = gate_up.shape
    hidden = down.shape[1]
    width = peers * features
    per = width // LANES
    blocks = 2 * CAP * per
    sources = recv.shape[0] // blocks
    me = place[0]
    tiles = 2 * hidden // LANES
    early, late = [], []
    for n, (piece, offset) in enumerate(zip(pieces, RING)):
        d = lax.rem(me + offset, peers)
        for i in range(tiles):
            early.append(
                pltpu.make_async_copy(
                    piece.at[pl.ds(i * LANES, LANES), :],
                    gate_up.at[d, :, pl.ds(i * LANES, LANES)],
                    in_sems.at[n, i],
                )
            )
        late.append(
            pltpu.make_async_copy(
                piece.at[pl.ds(2 * hidden, hidden), :], down.at[d], in_sems.at[n, tiles]
            )
        )
    for copy in early + late:
        copy.start()
    rows[...] = recv[...].astype(F32)
    x = jnp.concatenate(
        [gather_rows(rows, sources, r * per, blocks, per).astype(BF16) for r in range(CAP)], axis=0
    )
    g = jnp.concatenate(
        [gather_rows(rows, sources, (CAP + r) * per, blocks, per).astype(BF16) for r in range(CAP)],
        axis=0,
    )
    for copy in early:
        copy.wait()
    wide = gate_up[...].reshape(width, 2 * hidden)
    pre = dot(x, wide)
    gate_pre, up_pre = pre[:, :hidden], pre[:, hidden:]
    sigmoid = 1.0 / (1.0 + jnp.exp(-gate_pre))
    inner = (gate_pre * sigmoid * up_pre).astype(BF16)
    for copy in late:
        copy.wait()
    narrow = jnp.concatenate([down[d] for d in range(peers)], axis=1)
    hidden_grad = dot(g, narrow, ((1,), (1,)))
    out = dot(inner, narrow)
    for r in range(CAP):
        spread_rows(out[r * sources : (r + 1) * sources], rows, r * per, blocks)
    gate_grad = (hidden_grad * up_pre * sigmoid * (1.0 + gate_pre * (1.0 - sigmoid))).astype(BF16)
    up_grad = (hidden_grad * gate_pre * sigmoid).astype(BF16)
    both = jnp.concatenate([gate_grad, up_grad], axis=1)
    back_grad = dot(both, wide, ((1,), (1,)))
    for r in range(CAP):
        spread_rows(back_grad[r * sources : (r + 1) * sources], rows, (CAP + r) * per, blocks)
    leaving[...] = rows[...].astype(BF16)
    send_back = pltpu.make_async_copy(leaving, back, back_sem.at[0])
    send_back.start()
    down_full = dot(inner, g, ((0,), (0,))).astype(BF16)
    for d in range(peers):
        down_term[d] = down_full[:, d * features : (d + 1) * features]
    places = [lax.rem(me + offset, peers) for offset in range(peers)]
    copies = [
        pltpu.make_async_copy(
            down_term.at[d], ref.at[pl.ds(2 * hidden, hidden), :], out_sems.at[n, tiles]
        )
        for n, (ref, d) in enumerate(zip(terms, places))
    ]
    for copy in copies:
        copy.start()
    term[...] = dot(x, both, ((0,), (0,))).astype(BF16).reshape(term.shape)
    lines = [
        pltpu.make_async_copy(
            term.at[d, :, pl.ds(i * LANES, LANES)],
            ref.at[pl.ds(i * LANES, LANES), :],
            out_sems.at[n, i],
        )
        for n, (ref, d) in enumerate(zip(terms, places))
        for i in range(tiles)
    ]
    for copy in lines:
        copy.start()
    for copy in copies + lines:
        copy.wait()
    send_back.wait()


def combine_kernel(back, cotangent, ids, weights, layer, token_grads, router_grads, rows):
    tokens, width = cotangent.shape
    columns = ids.shape[0]
    per = width // LANES
    blocks = 2 * CAP * per
    experts = back.shape[0] // blocks
    rows[...] = back[...].astype(F32)
    matches, _, rank = token_ranks(ids[...], experts)
    ranks = [rank == float(r) for r in range(CAP)]
    values = weights[...].astype(F32)
    slots = [
        jnp.concatenate([jnp.where(match & at, 1.0, 0.0) for at in ranks], axis=0)
        for match in matches
    ]
    pairs = range(columns // 2)
    plain = jnp.concatenate([slots[2 * j] + slots[2 * j + 1] for j in pairs], axis=1).astype(BF16)
    scaled = jnp.concatenate(
        [
            slots[2 * j] * values[2 * j : 2 * j + 1, :]
            + slots[2 * j + 1] * values[2 * j + 1 : 2 * j + 2, :]
            for j in pairs
        ],
        axis=1,
    ).astype(BF16)
    outs = jnp.concatenate(
        [gather_rows(rows, experts, r * per, blocks, per).astype(BF16) for r in range(CAP)], axis=0
    )
    grads = jnp.concatenate(
        [
            gather_rows(rows, experts, (CAP + r) * per, blocks, per).astype(BF16)
            for r in range(CAP)
        ],
        axis=0,
    )
    out = dot(scaled, outs, ((0,), (0,))).astype(BF16).astype(F32)
    grad = dot(plain, grads, ((0,), (0,))).astype(BF16).astype(F32)
    total, total_grad = out[:tokens], grad[:tokens]
    for j in pairs[1:]:
        total = total + out[j * tokens : (j + 1) * tokens]
        total_grad = total_grad + grad[j * tokens : (j + 1) * tokens]
    layer[...] = total.astype(BF16)
    token_grads[...] = total_grad.astype(BF16)
    products = dot(outs, cotangent[...], ((1,), (1,)))
    row = lax.broadcasted_iota(jnp.int32, (columns, tokens), 0)
    routed = jnp.zeros((columns, tokens), F32)
    for k, slot in enumerate(slots):
        column = jnp.sum(slot * products, axis=0, keepdims=True)
        routed = jnp.where(row == k, column, routed)
    router_grads[...] = routed.astype(BF16)


def finish_kernel(back, right, left, own, cotangent, ids, weights, *refs):
    layer, token_grads, router_grads, gate, up, down, mine, rows, sem = refs
    copy = pltpu.make_async_copy(own, mine, sem.at[0])
    copy.start()
    combine_kernel(back, cotangent, ids, weights, layer, token_grads, router_grads, rows)
    copy.wait()
    features, hidden = gate.shape
    total = (
        mine[...].astype(F32) + right[...].astype(F32) + left[...].astype(F32)
    ).astype(BF16)
    for i, weight in enumerate((gate, up)):
        for c in range(hidden // LANES):
            at = i * hidden + c * LANES
            weight[:, c * LANES : (c + 1) * LANES] = total[at : at + features, :]
    down[...] = total[2 * hidden :, :]


def call(kernel, outs, scratch=(), in_specs=None):
    shapes = [jax.ShapeDtypeStruct(shape, BF16) for shape in outs]
    single = len(shapes) == 1
    return pl.pallas_call(
        kernel,
        out_shape=shapes[0] if single else shapes,
        in_specs=in_specs,
        out_specs=vmem() if single else [vmem() for _ in shapes],
        scratch_shapes=list(scratch),
        interpret=INTERPRET,
    )


def prepare(tokens, cotangent, ids, weights, gate, up, down, experts):
    lines = experts * 2 * CAP * tokens.shape[1] // LANES
    return call(
        prepare_kernel,
        [(lines, LANES), (3 * gate.shape[1], LANES)],
        scratch=[pltpu.VMEM((lines, LANES), F32)],
        in_specs=[vmem()] * 7,
    )(tokens, cotangent, ids, weights, gate, up, down)


def expert(place, recv, pieces, hidden, width):
    peers = width // LANES
    lines = pieces[0].shape[0]
    anywhere = pl.BlockSpec(memory_space=pl.ANY)
    copies = 2 * hidden // LANES + 1
    return pl.pallas_call(
        expert_kernel,
        out_shape=[jax.ShapeDtypeStruct(recv.shape, BF16)]
        + [jax.ShapeDtypeStruct((lines, LANES), BF16)] * peers,
        in_specs=[pl.BlockSpec(memory_space=pltpu.SMEM), vmem()] + [anywhere] * peers,
        out_specs=[anywhere] * (1 + peers),
        scratch_shapes=[
            pltpu.VMEM(recv.shape, F32),
            pltpu.VMEM((peers, LANES, 2 * hidden), BF16),
            pltpu.VMEM((peers, hidden, LANES), BF16),
            pltpu.VMEM((peers, LANES, 2 * hidden), BF16),
            pltpu.VMEM((peers, hidden, LANES), BF16),
            pltpu.VMEM(recv.shape, BF16),
            pltpu.SemaphoreType.DMA((peers, copies)),
            pltpu.SemaphoreType.DMA((peers, copies)),
            pltpu.SemaphoreType.DMA((1,)),
        ],
        interpret=INTERPRET,
        name="expert",
    )(place, recv, *pieces)


def shifted(value, by):
    peers = lax.axis_size("dp")
    return lax.ppermute(value, "dp", [(i, (i + by) % peers) for i in range(peers)])


def gather_ring(chunk):
    right, left = [chunk], [chunk]
    for _ in range(4):
        right.append(shifted(right[-1], 1))
    for _ in range(3):
        left.append(shifted(left[-1], -1))
    return right + left[1:]


def scatter_ring(terms):
    right = shifted(terms[4], 1)
    left = shifted(terms[5], -1)
    for step in (1, 2, 3):
        right = shifted(terms[4 - step] + right, 1)
        if step < 3:
            left = shifted(terms[5 + step] + left, -1)
    return terms[0], right, left


def finish(back, cotangent, ids, weights, parts, features, hidden):
    anywhere = pl.BlockSpec(memory_space=pl.ANY)
    return call(
        finish_kernel,
        [
            cotangent.shape,
            cotangent.shape,
            ids.shape,
            (features, hidden),
            (features, hidden),
            (hidden, LANES),
        ],
        scratch=[
            pltpu.VMEM(parts[0].shape, BF16),
            pltpu.VMEM(back.shape, F32),
            pltpu.SemaphoreType.DMA((1,)),
        ],
        in_specs=[vmem()] * 3 + [anywhere] + [vmem()] * 3,
    )(on_chip(back), on_chip(parts[1]), on_chip(parts[2]), parts[0], cotangent, ids, weights)


def on_chip(value):
    return value if INTERPRET else pltpu.with_memory_space_constraint(value, pltpu.VMEM)


def exchange(lines, peers):
    out = lax.all_to_all(
        lines.reshape(peers, -1, LANES),
        ("group", "local"),
        split_axis=0,
        concat_axis=0,
        tiled=True,
    )
    return out.reshape(lines.shape)


def local(tokens, cotangent, expert_ids, router_weights, gate_weight, up_weight, down_weight):
    experts = lax.axis_size("group") * lax.axis_size("local")
    features, hidden = gate_weight.shape[1:]
    width = tokens.shape[1]
    ids, weights = expert_ids.T, router_weights.T
    sent, packed = prepare(
        tokens, cotangent, ids, weights, gate_weight[0], up_weight[0], down_weight[0], experts
    )
    recv = exchange(sent, experts)
    pieces = gather_ring(packed)
    place = lax.axis_index("dp").astype(jnp.int32).reshape(1)
    back, *terms = expert(place, on_chip(recv), pieces, hidden, width)
    returned = exchange(back, experts)
    parts = scatter_ring(terms)
    layer, token_grads, router_grads, gate, up, down = finish(
        returned, cotangent, ids, weights, parts, features, hidden
    )
    return layer, token_grads, router_grads.T, gate[None], up[None], down[None]


def solution(mesh):
    tokens = P(("dp", "group", "local"), None)
    rows = P(("group", "local"), "dp", None)
    columns = P(("group", "local"), None, "dp")
    return jax.shard_map(
        local,
        mesh=mesh,
        in_specs=(tokens, tokens, tokens, tokens, rows, rows, columns),
        out_specs=(tokens, tokens, tokens, rows, rows, columns),
        check_vma=False,
    )
```
